32 devices in a mesh: ens: 8 (over y, x, core), lon: 4 (over z).
Axes of the slice: x: 2, y: 2, z: 4, core: 2. Of those that a mesh axis runs over, the one named last changes fastest.
Arguments:
- features: bfloat16 [8, 384, 46080], P('ens', None, 'lon'), may hold values from -6 to 6
- proj_weight: bfloat16 [648, 384], replicated, may hold values from -0.3125 to 0.3125
- basis_vals: float32 [32, 32, 9], replicated, may hold values from -0.375 to 0.375
- row_of: int32 [32, 32], replicated, may hold values from 0 to 31
- col_off: int32 [32, 32], replicated, may hold values from -4 to 4
- observed: float32 [72, 46080], P(None, 'lon'), may hold values from -6 to 6
- lat_weight: float32 [32], replicated, may hold values from 0.3 to 1
Outputs:
- feature_grad: bfloat16 [8, 384, 46080], P('ens', None, 'lon')
- weight_grad: float32 [648, 384], replicated
The draws below stay inside these ranges and needn't reach their ends.
Inputs may be any that keep to these rules, and one draw needn't show every extreme that they name: row_of names a row of the slab. col_off is a longitude offset in columns.
All inputs are finite; a program needn't handle non-finite values.
Results may differ from the reference program's by a relative error of at most 0.0089.
Values may be sent and summed in bfloat16 or wider, within the bound.
A program may use at most 256 MiB of HBM per device.

```python
import math
import jax
import jax.numpy as jnp
from jax import lax

C = 384
O = 72
NLON = 1440
K = 9
S = 32
R = 4
LAT = 32
MEMBERS = 8


def set_ends(entries, stream_key, low, largest):
    shape = entries.shape
    spot = [jax.random.randint(jax.random.fold_in(stream_key, axis), (), 0, shape[axis]) for axis in range(len(shape))]
    entries = entries.at[tuple(spot)].set(low)
    longest = shape.index(max(shape))
    spot[longest] = (spot[longest] + 1) % shape[longest]
    return entries.at[tuple(spot)].set(largest)


def block_scale(key, dims, pieces, least, high):
    level = 1.0
    for position, shards_of in pieces:
        draws = jax.random.uniform(jax.random.fold_in(jax.random.fold_in(key, 6), position), (shards_of,), jnp.float32, least / len(pieces), high / len(pieces))
        level = level * jnp.repeat(jnp.exp(draws), dims[position] // shards_of).reshape((-1,) + (1,) * (len(dims) - 1 - position))
    return level


def normal_values(own_key, shape, deviation, bound, shards=(), kind=jnp.bfloat16):
    array = deviation * jax.random.normal(own_key, shape, jnp.float32)
    if shards:
        array = array * block_scale(own_key, shape, shards, -0.22, 0.18)
    return jnp.clip(array, -bound, bound).astype(kind)


def setup_inputs(seed: int = 0) -> dict:
    streams_of = jax.random.split(jax.random.key(seed), 8)
    features = normal_values(streams_of[0], (MEMBERS, C, NLON * LAT), 1.0, 6.0, ((0, 8), (2, 4)))
    proj_weight = normal_values(streams_of[1], (K * O, C), C ** -0.5, 0.3125)
    basis_vals = normal_values(streams_of[2], (LAT, S, K), (S * K) ** -0.5, 0.375, (), jnp.float32)
    row_of = set_ends(jax.random.randint(streams_of[3], (LAT, S), 0, LAT), jax.random.fold_in(streams_of[3], 1), 0, LAT - 1).astype(jnp.int32)
    col_off = set_ends(jax.random.randint(streams_of[4], (LAT, S), 0 - R, R + 1), jax.random.fold_in(streams_of[4], 1), 0 - R, R).astype(jnp.int32)
    observed = normal_values(streams_of[5], (O, NLON * LAT), 1.0, 6.0, ((1, 4),), jnp.float32)
    lat_weight = jnp.clip(jnp.exp(jax.random.uniform(streams_of[6], (LAT,), jnp.float32, math.log(0.3), math.log(1.0))), 0.3, 1.0)
    return dict(features=features, proj_weight=proj_weight, basis_vals=basis_vals, row_of=row_of, col_off=col_off, observed=observed, lat_weight=lat_weight)


SMOOTH = 0.25

def kernel_table(basis_vals, row_of, col_off):
    offsets = jnp.arange(2 * R + 1, dtype=jnp.int32) - R
    row_ids = jnp.arange(LAT, dtype=jnp.int32)
    row_hit = (row_of[:, :, None] == row_ids[None, None, :]).astype(jnp.float32)
    col_hit = (col_off[:, :, None] == offsets[None, None, :]).astype(jnp.float32)
    kernel = jnp.einsum('isk,isr,isd->dkir', basis_vals.astype(jnp.float32), row_hit, col_hit, precision=lax.Precision.HIGHEST)
    return kernel.astype(jnp.bfloat16)

def smooth_slope(diff):
    return diff / jnp.sqrt(diff * diff + SMOOTH * SMOOTH)

def reference(features, proj_weight, basis_vals, row_of, col_off, observed, lat_weight):
    kernel = lax.optimization_barrier(kernel_table(basis_vals, row_of, col_off)).astype(jnp.float32)
    weight_wide = proj_weight.astype(jnp.float32)

    def forward(member):
        projected = jnp.dot(weight_wide, member.astype(jnp.float32), precision=lax.Precision.HIGHEST).astype(jnp.bfloat16)
        projected = lax.optimization_barrier(projected).astype(jnp.float32).reshape(K, O, NLON, LAT)
        decoded = jnp.zeros((O, NLON, LAT), jnp.float32)
        for offset in range(2 * R + 1):
            decoded = decoded + jnp.einsum('kir,kojr->oji', kernel[offset], jnp.roll(projected, R - offset, axis=2), precision=lax.Precision.HIGHEST)
        return decoded
    outputs = lax.map(forward, features)
    target = observed.reshape(O, NLON, LAT)

    def member_grad(own_row):
        spread = lax.optimization_barrier(jnp.sum(smooth_slope(own_row[None] - outputs), axis=0))
        return smooth_slope(own_row - target) - spread / (MEMBERS - 1)
    slopes = lax.map(member_grad, outputs)
    cotangent = lax.optimization_barrier((slopes * lat_weight).astype(jnp.bfloat16))

    def backward(paired):
        member, cot_member = paired
        cot_wide = cot_member.astype(jnp.float32)
        spread_grad = jnp.zeros((K, O, NLON, LAT), jnp.float32)
        for offset in range(2 * R + 1):
            spread_grad = spread_grad + jnp.einsum('kir,oji->kojr', kernel[offset], jnp.roll(cot_wide, offset - R, axis=1), precision=lax.Precision.HIGHEST)
        spread_grad = spread_grad.reshape(K * O, NLON * LAT).astype(jnp.bfloat16)
        spread_grad = lax.optimization_barrier(spread_grad).astype(jnp.float32)
        feature_grad = jnp.dot(weight_wide.T, spread_grad, precision=lax.Precision.HIGHEST).astype(jnp.bfloat16)
        weight_part = jnp.dot(spread_grad, member.astype(jnp.float32).T, precision=lax.Precision.HIGHEST)
        return (feature_grad, weight_part)
    feature_grads, weight_parts = lax.map(backward, (features, cotangent))
    weight_grad = lax.optimization_barrier(jnp.sum(weight_parts, axis=0)) / math.sqrt(MEMBERS * NLON * LAT)
    return (feature_grads, weight_grad)
```

```python
import functools
import math

import jax
import jax.numpy as jnp
from jax import lax
from jax.experimental import pallas as pl
from jax.experimental.pallas import tpu as pltpu
from jax.sharding import PartitionSpec as P

O = 72
OP = 80
K = 9
R = 4
LAT = 32
SMOOTH = 0.25
BLK = 256
HALF = 128
F32 = jnp.float32
BF16 = jnp.bfloat16
MESH = pl.DeviceIdType.MESH
VMEM_LIMIT = 60 * 1024 * 1024


def whole(shape):
    return pl.BlockSpec(shape, lambda s: (0,) * len(shape))


def kernel_rows(basis_vals, row_of, col_off):
    code = (col_off + R) * LAT + row_of
    ids = jnp.arange((2 * R + 1) * LAT, dtype=jnp.int32)
    hit = (code[:, :, None] == ids[None, None, :]).astype(F32)
    table = jnp.einsum("isk,isq->ikq", basis_vals, hit, precision=lax.Precision.HIGHEST)
    return table.astype(BF16)


def band_tables(table):
    taps = 2 * R + 1
    cols = BLK // LAT
    four = table.reshape(LAT, K, taps, LAT)
    ahead = four.transpose(1, 2, 3, 0)
    back = four[:, :, ::-1].transpose(1, 2, 0, 3)
    out = []
    for base in (ahead, back):
        parts = [
            jnp.pad(base, ((0, 0), (j, 2 * cols - taps - j), (0, 0), (0, 0))).reshape(
                K, 2 * BLK, LAT
            )
            for j in range(cols)
        ]
        out.append(jnp.concatenate(parts, axis=2))
    return out


def forward_kernel(group, steps, feat, left, right, weight, band, out, proj):
    s = pl.program_id(0)

    def put(values, h, lo):
        for k in range(K):
            proj[k, h, :, lo : lo + HALF] = values[k * OP : (k + 1) * OP].astype(BF16)

    @pl.when(s == 0)
    def _():
        put(jnp.dot(weight[...], left[...], preferred_element_type=F32), 0, 0)

    @pl.when(s < steps)
    def _():
        def one(n, carry):
            lanes = pl.ds(pl.multiple_of(n * BLK, BLK), BLK)
            got = jnp.dot(weight[...], feat[:, lanes], preferred_element_type=F32)
            h = s * group + n
            put(got[:, :HALF], h, HALF)
            put(got[:, HALF:], h + 1, 0)
            return carry

        lax.fori_loop(0, group, one, 0)

    @pl.when(s == steps)
    def _():
        put(jnp.dot(weight[...], right[...], preferred_element_type=F32), steps * group, HALF)

    @pl.when(s > 0)
    def _():
        g0 = (s - 1) * group
        acc = jnp.zeros((group * OP, BLK), F32)
        for k in range(K):
            for part in range(2):
                lhs = proj[k, pl.ds(g0 + part, group)].reshape(group * OP, BLK)
                acc = acc + jnp.dot(
                    lhs, band[k, part * BLK : (part + 1) * BLK, :], preferred_element_type=F32
                )
        for g in range(group):
            piece = acc[g * OP : g * OP + O]
            both = jnp.concatenate([piece[:, :HALF], piece[:, HALF:]], axis=0)
            out[g * 2 * O : (g + 1) * 2 * O, :] = both.astype(BF16)


def forward(feat, left, right, weight, band, group, steps, rows):
    chan = feat.shape[0]
    wide = group * BLK
    return pl.pallas_call(
        functools.partial(forward_kernel, group, steps),
        out_shape=jax.ShapeDtypeStruct((rows, HALF), BF16),
        grid=(steps + 1,),
        in_specs=[
            pl.BlockSpec((chan, wide), lambda s: (0, jnp.minimum(s, steps - 1))),
            whole(left.shape),
            whole(right.shape),
            whole(weight.shape),
            whole(band.shape),
        ],
        out_specs=pl.BlockSpec((group * 2 * O, HALF), lambda s: (jnp.maximum(s - 1, 0), 0)),
        scratch_shapes=[pltpu.VMEM((K, steps * group + 1, OP, BLK), BF16)],
        compiler_params=pltpu.CompilerParams(vmem_limit_bytes=VMEM_LIMIT),
        name="forward_conv",
    )(feat, left, right, weight, band)


def greet(peers):
    barrier = pltpu.get_barrier_semaphore()
    for peer in peers:
        pl.semaphore_signal(barrier, inc=1, device_id=peer, device_id_type=MESH)
    pl.semaphore_wait(barrier, len(peers))


def slope_kernel(n, dec, obs, lat, cot, recv, send, ssem1, rsem1, ssem2, rsem2):
    me = lax.axis_index("ens")
    rows = obs.shape[0]
    greet([{"ens": lax.rem(me + off, n)} for off in range(1, n)])
    first = []
    for off in range(1, n):
        peer = lax.rem(me + off, n)
        copy = pltpu.make_async_remote_copy(
            src_ref=dec.at[pl.ds(pl.multiple_of(peer * rows, 16), rows)],
            dst_ref=recv.at[off],
            send_sem=ssem1.at[off],
            recv_sem=rsem1.at[off],
            device_id={"ens": peer},
            device_id_type=MESH,
        )
        copy.start()
        first.append(copy)
    for copy in first:
        copy.wait()
    own = pl.multiple_of(me * rows, 16)
    lat_row = jnp.broadcast_to(lat[0:1, :], (16, HALF))

    def smooth(diff):
        return diff * lax.rsqrt(diff * diff + SMOOTH * SMOOTH)

    def one(step, carry):
        at = pl.multiple_of(step * 16, 16)
        values = [dec[pl.ds(pl.multiple_of(own + at, 16), 16), :].astype(F32)]
        values += [recv[off, pl.ds(at, 16), :].astype(F32) for off in range(1, n)]
        sums = [None] * n
        for a in range(n):
            for b in range(a + 1, n):
                pair = smooth(values[a] - values[b])
                sums[a] = pair if sums[a] is None else sums[a] + pair
                sums[b] = -pair if sums[b] is None else sums[b] - pair
        target = obs[pl.ds(at, 16), :]
        for a in range(n):
            slope = smooth(values[a] - target) - sums[a] * (1.0 / (n - 1))
            result = (slope * lat_row).astype(BF16)
            if a == 0:
                cot[pl.ds(pl.multiple_of(own + at, 16), 16), :] = result
            else:
                send[a, pl.ds(at, 16), :] = result
        return carry

    lax.fori_loop(0, rows // 16, one, 0)
    second = []
    for off in range(1, n):
        peer = lax.rem(me - off + n, n)
        copy = pltpu.make_async_remote_copy(
            src_ref=send.at[off],
            dst_ref=cot.at[pl.ds(own, rows)],
            send_sem=ssem2.at[off],
            recv_sem=rsem2.at[off],
            device_id={"ens": peer},
            device_id_type=MESH,
        )
        copy.start()
        second.append(copy)
    for copy in second:
        copy.wait()


def slopes(n, dec, obs, lat):
    rows = obs.shape[0]
    vmem = pl.BlockSpec(memory_space=pltpu.VMEM)
    return pl.pallas_call(
        functools.partial(slope_kernel, n),
        out_shape=jax.ShapeDtypeStruct(dec.shape, BF16),
        in_specs=[vmem] * 3,
        out_specs=vmem,
        scratch_shapes=[
            pltpu.VMEM((n, rows, HALF), BF16),
            pltpu.VMEM((n, rows, HALF), BF16),
            pltpu.SemaphoreType.DMA((n,)),
            pltpu.SemaphoreType.DMA((n,)),
            pltpu.SemaphoreType.DMA((n,)),
            pltpu.SemaphoreType.DMA((n,)),
        ],
        compiler_params=pltpu.CompilerParams(
            collective_id=0, has_side_effects=True, vmem_limit_bytes=VMEM_LIMIT
        ),
        name="member_slopes",
    )(dec, obs, lat)


WG_ROWS = 2048
WG_PART = 656


def backward_kernel(
    group, steps, cells, padded, cot, left, right, weight_t, band, feat, grad, wgrad, ext, spread, acc
):
    s = pl.program_id(0)
    blocks = steps * group

    @pl.when(s == 0)
    def _():
        ext[:, O:, :] = jnp.zeros((blocks + 1, OP - O, BLK), BF16)
        ext[0, :O, :HALF] = left[...]
        ext[blocks, :O, HALF:] = right[...]

        def one(b, carry):
            pair = cot[pl.ds(pl.multiple_of(b * 2 * O, 16), 2 * O), :].astype(F32)
            ext[b, :O, HALF:] = pair[:O].astype(BF16)
            ext[b + 1, :O, :HALF] = pair[O:].astype(BF16)
            return carry

        lax.fori_loop(0, blocks, one, 0)
        acc[...] = jnp.zeros_like(acc)

    g0 = s * group
    for k in range(K):
        got = jnp.zeros((group * OP, BLK), F32)
        for part in range(2):
            lhs = ext[pl.ds(g0 + part, group)].reshape(group * OP, BLK)
            got = got + jnp.dot(
                lhs, band[k, part * BLK : (part + 1) * BLK, :], preferred_element_type=F32
            )
        if padded:
            row = lax.broadcasted_iota(jnp.int32, got.shape, 0) // OP
            lane = lax.broadcasted_iota(jnp.int32, got.shape, 1)
            got = jnp.where((g0 + row) * BLK + lane < cells, got, 0.0)
        got = got.astype(BF16)
        for g in range(group):
            spread[k * OP : (k + 1) * OP, g * BLK : (g + 1) * BLK] = got[g * OP : (g + 1) * OP]

    acc[...] += lax.dot_general(
        spread[...], feat[...], (((1,), (1,)), ((), ())), preferred_element_type=F32
    )

    def one_grad(n, carry):
        lanes = pl.ds(pl.multiple_of(n * BLK, BLK), BLK)
        grad[:, lanes] = jnp.dot(
            weight_t[...], spread[:, lanes], preferred_element_type=F32
        ).astype(BF16)
        return carry

    lax.fori_loop(0, group, one_grad, 0)

    @pl.when(s == steps - 1)
    def _():
        parts = acc.shape[1] // HALF
        wgrad[parts * WG_PART - 16 :, :] = jnp.zeros((WG_ROWS - parts * WG_PART + 16, HALF), BF16)
        for t in range(parts):
            rows = [
                acc[k * OP : k * OP + O, t * HALF : (t + 1) * HALF] for k in range(K)
            ] + [jnp.zeros((8, HALF), F32)]
            wgrad[t * WG_PART : (t + 1) * WG_PART, :] = jnp.concatenate(rows, axis=0).astype(BF16)


def backward(cot, left, right, weight_t, band, feat, group, steps, cells):
    chan = feat.shape[0]
    wide = group * BLK
    blocks = steps * group
    return pl.pallas_call(
        functools.partial(backward_kernel, group, steps, cells, cells != blocks * BLK),
        out_shape=(
            jax.ShapeDtypeStruct(feat.shape, BF16),
            jax.ShapeDtypeStruct((WG_ROWS, HALF), BF16),
        ),
        grid=(steps,),
        in_specs=[
            whole(cot.shape),
            whole(left.shape),
            whole(right.shape),
            whole(weight_t.shape),
            whole(band.shape),
            pl.BlockSpec((chan, wide), lambda s: (0, s)),
        ],
        out_specs=(pl.BlockSpec((chan, wide), lambda s: (0, s)), whole((WG_ROWS, HALF))),
        scratch_shapes=[
            pltpu.VMEM((blocks + 1, OP, BLK), BF16),
            pltpu.VMEM((K * OP, wide), BF16),
            pltpu.VMEM((K * OP, chan), F32),
        ],
        compiler_params=pltpu.CompilerParams(vmem_limit_bytes=VMEM_LIMIT),
        name="backward_conv",
    )(cot, left, right, weight_t, band, feat)


def reduce_kernel(ne, nl, scale, part, out, recv1, mid, recv2, got, *sems):
    (ss1, rs1, ss2, rs2, ss3, rs3, ss4, rs4) = sems
    me = lax.axis_index("ens")
    at = lax.axis_index("lon")
    rows = WG_ROWS // ne
    small = rows // nl
    ens_peers = [{"ens": lax.rem(me + off, ne)} for off in range(1, ne)]
    lon_peers = [{"lon": lax.rem(at + off, nl)} for off in range(1, nl)]
    greet(ens_peers + lon_peers)

    def run(copies):
        for copy in copies:
            copy.start()
        for copy in copies:
            copy.wait()

    def send(src, dst, ssem, rsem, peer):
        return pltpu.make_async_remote_copy(
            src_ref=src, dst_ref=dst, send_sem=ssem, recv_sem=rsem, device_id=peer, device_id_type=MESH
        )

    own = pl.multiple_of(me * rows, 16)
    mine = pl.multiple_of(at * small, 8)
    run(
        [
            send(
                part.at[pl.ds(pl.multiple_of(lax.rem(me + off, ne) * rows, 16), rows)],
                recv1.at[off],
                ss1.at[off],
                rs1.at[off],
                {"ens": lax.rem(me + off, ne)},
            )
            for off in range(1, ne)
        ]
    )
    total = part[pl.ds(own, rows), :].astype(F32)
    for off in range(1, ne):
        total = total + recv1[off].astype(F32)
    mid[...] = total
    run(
        [
            send(
                mid.at[pl.ds(pl.multiple_of(lax.rem(at + off, nl) * small, 8), small)],
                recv2.at[off],
                ss2.at[off],
                rs2.at[off],
                {"lon": lax.rem(at + off, nl)},
            )
            for off in range(1, nl)
        ]
    )
    total = mid[pl.ds(mine, small), :]
    for off in range(1, nl):
        total = total + recv2[off]
    recv2[0] = total
    gat = got[1]
    gat[pl.ds(mine, small), :] = total
    run(
        [
            send(
                recv2.at[0],
                gat.at[pl.ds(mine, small)],
                ss3.at[off],
                rs3.at[off],
                {"lon": lax.rem(at + off, nl)},
            )
            for off in range(1, nl)
        ]
    )
    full = got[0]
    full[pl.ds(own, rows), :] = gat[...].astype(BF16)
    run(
        [
            send(
                full.at[pl.ds(own, rows)],
                full.at[pl.ds(own, rows)],
                ss4.at[off],
                rs4.at[off],
                {"ens": lax.rem(me + off, ne)},
            )
            for off in range(1, ne)
        ]
    )
    for t in range(out.shape[1] // HALF):
        piece = full[t * WG_PART : (t + 1) * WG_PART, :].astype(F32) * scale
        out[:, t * HALF : (t + 1) * HALF] = piece[: K * O]


def reduced(ne, nl, scale, part, chan):
    vmem = pl.BlockSpec(memory_space=pltpu.VMEM)
    rows = WG_ROWS // ne
    small = rows // nl

    def body(part, out, recv1, mid, recv2, full, gat, *sems):
        reduce_kernel(ne, nl, scale, part, out, recv1, mid, recv2, (full, gat), *sems)

    return pl.pallas_call(
        body,
        out_shape=jax.ShapeDtypeStruct((K * O, chan), F32),
        in_specs=[vmem],
        out_specs=vmem,
        scratch_shapes=[
            pltpu.VMEM((ne, rows, HALF), BF16),
            pltpu.VMEM((rows, HALF), F32),
            pltpu.VMEM((nl, small, HALF), F32),
            pltpu.VMEM((WG_ROWS, HALF), BF16),
            pltpu.VMEM((rows, HALF), F32),
        ]
        + [pltpu.SemaphoreType.DMA((n,)) for n in (ne, ne, nl, nl, nl, nl, ne, ne)],
        compiler_params=pltpu.CompilerParams(
            collective_id=1, has_side_effects=True, vmem_limit_bytes=VMEM_LIMIT
        ),
        name="weight_reduce",
    )(part)


def passed_along(value, axis, steps):
    count = lax.axis_size(axis)
    return lax.ppermute(value, axis, [(i, (i + steps) % count) for i in range(count)])


def shards(features, proj_weight, basis_vals, row_of, col_off, observed, lat_weight):
    ne = lax.axis_size("ens")
    nl = lax.axis_size("lon")
    assert features.shape[0] == 1
    feat = features[0]
    chan, cells = feat.shape
    aligned = cells % BLK == 0
    blocks = cells // BLK if aligned else pl.cdiv(cells + HALF, BLK)
    group = max(g for g in range(1, 10) if blocks % g == 0)
    steps = blocks // group
    tiles = 2 * blocks
    per = pl.cdiv(tiles, ne)
    per += per % 2
    rows = per * ne * O
    extra = blocks * BLK - cells

    left = passed_along(feat[:, cells - HALF :], "lon", 1)
    right = passed_along(feat[:, :HALF], "lon", -1)
    ahead, back = band_tables(kernel_rows(basis_vals, row_of, col_off))
    weight = jnp.pad(proj_weight.reshape(K, O, chan), ((0, 0), (0, OP - O), (0, 0)))
    weight = weight.reshape(K * OP, chan)
    if not aligned:
        feat = jnp.pad(jnp.concatenate([feat, right], axis=1), ((0, 0), (0, extra - HALF)))
        right = jnp.zeros_like(right)
    dec = forward(feat, left, right, weight, ahead, group, steps, rows)

    obs = jnp.pad(observed, ((0, 0), (0, per * ne * HALF - cells)))
    obs = lax.dynamic_slice_in_dim(obs, lax.axis_index("ens") * per * HALF, per * HALF, axis=1)
    obs = obs.reshape(O, per, HALF).transpose(1, 0, 2).reshape(per * O, HALF)
    lat = jnp.broadcast_to(jnp.tile(lat_weight, HALF // LAT)[None, :], (8, HALF))
    cot = slopes(ne, dec, obs, lat)

    if aligned:
        cot_left = passed_along(cot[(tiles - 1) * O : tiles * O], "lon", 1)
        cot_right = passed_along(cot[:O], "lon", -1)
    else:
        flat = cot.reshape(per * ne, O, HALF).transpose(1, 0, 2).reshape(O, per * ne * HALF)
        flat = flat[:, :cells]
        cot_left = passed_along(flat[:, cells - HALF :], "lon", 1)
        cot_right = passed_along(flat[:, :HALF], "lon", -1)
        flat = jnp.pad(
            jnp.concatenate([flat, cot_right], axis=1),
            ((0, 0), (0, per * ne * HALF - cells - HALF)),
        )
        cot = flat.reshape(O, per * ne, HALF).transpose(1, 0, 2).reshape(rows, HALF)
        cot_right = jnp.zeros_like(cot_right)
    grad, part = backward(cot, cot_left, cot_right, weight.T, back, feat, group, steps, cells)
    scale = 1.0 / math.sqrt(ne * (cells // LAT) * nl * LAT)
    weight_grad = reduced(ne, nl, scale, part, chan)
    return (grad[:, :cells][None], weight_grad)


def solution(mesh):
    in_specs = (P("ens", None, "lon"), P(), P(), P(), P(), P(None, "lon"), P())
    out_specs = (P("ens", None, "lon"), P())
    return jax.shard_map(shards, mesh=mesh, in_specs=in_specs, out_specs=out_specs, check_vma=False)
```

```python
import functools
import math

import jax
import jax.numpy as jnp
from jax import lax
from jax.experimental import pallas as pl
from jax.experimental.pallas import tpu as pltpu
from jax.sharding import PartitionSpec as P

O = 72
OP = 80
K = 9
R = 4
LAT = 32
SMOOTH = 0.25
BLK = 256
HALF = 128
F32 = jnp.float32
BF16 = jnp.bfloat16
MESH = pl.DeviceIdType.MESH
VMEM_LIMIT = 60 * 1024 * 1024


def whole(shape):
    return pl.BlockSpec(shape, lambda s: (0,) * len(shape))


def kernel_rows(basis_vals, row_of, col_off):
    code = (col_off + R) * LAT + row_of
    ids = jnp.arange((2 * R + 1) * LAT, dtype=jnp.int32)
    hit = (code[:, :, None] == ids[None, None, :]).astype(F32)
    table = jnp.einsum("isk,isq->ikq", basis_vals, hit, precision=lax.Precision.HIGHEST)
    return table.astype(BF16)


def side_tables(table):
    taps = 2 * R + 1
    four = table.reshape(LAT, K, taps, LAT)
    ahead = four.transpose(1, 2, 3, 0).reshape(K, taps * LAT, LAT)
    back = four[:, :, ::-1].transpose(1, 2, 0, 3).reshape(K, taps * LAT, LAT)
    return ahead, back


def build_band(table, band):
    lane = lax.broadcasted_iota(jnp.int32, (LAT, BLK), 1)
    spread_lanes = (lane % LAT == lax.broadcasted_iota(jnp.int32, (LAT, BLK), 0)).astype(F32)
    spread_lanes = spread_lanes.astype(BF16)
    place = lane // LAT
    cols = BLK // LAT

    def one(k, carry):
        tiled = jnp.dot(table[k], spread_lanes, preferred_element_type=F32)
        for e in range(2 * cols):
            block = jnp.zeros((LAT, BLK), F32)
            for j in range(cols):
                d = e - j
                if 0 <= d <= 2 * R:
                    block = jnp.where(place == j, tiled[d * LAT : (d + 1) * LAT], block)
            band[k, e * LAT : (e + 1) * LAT, :] = block.astype(BF16)
        return carry

    lax.fori_loop(0, K, one, 0)


def padded_weight(weight):
    wide = weight[...].astype(F32)
    gap = jnp.zeros((OP - O, wide.shape[1]), F32)
    rows = []
    for k in range(K):
        rows += [wide[k * O : (k + 1) * O], gap]
    return jnp.concatenate(rows, axis=0)


def greet(peers):
    barrier = pltpu.get_barrier_semaphore()
    for peer in peers:
        pl.semaphore_signal(barrier, inc=1, device_id=peer, device_id_type=MESH)
    pl.semaphore_wait(barrier, len(peers))


def forward_kernel(
    n, group, steps, share,
    feat, left, right, weight, table, obs, lat, out,
    wpad, band, proj, dec, flat, recv, send, cot, ssem1, rsem1, ssem2, rsem2,
):
    s = pl.program_id(0)
    me = lax.axis_index("ens")
    real = group * 2 * O
    own = pl.multiple_of(me * share, 16)

    def first(q, off):
        peer = lax.rem(me + off, n)
        return pltpu.make_async_remote_copy(
            src_ref=dec.at[q, pl.ds(pl.multiple_of(peer * share, 16), share)],
            dst_ref=recv.at[q, off],
            send_sem=ssem1.at[q, off],
            recv_sem=rsem1.at[q, off],
            device_id={"ens": peer},
            device_id_type=MESH,
        )

    def second(q, off):
        return pltpu.make_async_remote_copy(
            src_ref=send.at[q, off],
            dst_ref=cot.at[q, pl.ds(own, share)],
            send_sem=ssem2.at[q, off],
            recv_sem=rsem2.at[q, off],
            device_id={"ens": lax.rem(me - off + n, n)},
            device_id_type=MESH,
        )

    def put(values, h, lo):
        for k in range(K):
            proj[k, h, :, lo : lo + HALF] = values[k * OP : (k + 1) * OP].astype(BF16)

    @pl.when(s == 0)
    def _():
        greet([{"ens": lax.rem(me + off, n)} for off in range(1, n)])
        wpad[...] = padded_weight(weight).astype(BF16)
        build_band(table, band)
        if n * share > real:
            for q in range(steps):
                dec[q, real:, :] = jnp.zeros((n * share - real, HALF), BF16)
            flat[real:, :] = jnp.zeros((n * share - real, HALF), F32)
        put(jnp.dot(wpad[...], left[...], preferred_element_type=F32), 0, 0)

    @pl.when(s < steps)
    def _():
        def one(b, carry):
            lanes = pl.ds(pl.multiple_of(b * BLK, BLK), BLK)
            got = jnp.dot(wpad[...], feat[:, lanes], preferred_element_type=F32)
            h = s * group + b
            put(got[:, :HALF], h, HALF)
            put(got[:, HALF:], h + 1, 0)
            return carry

        lax.fori_loop(0, group, one, 0)

    @pl.when(s == steps)
    def _():
        put(jnp.dot(wpad[...], right[...], preferred_element_type=F32), steps * group, HALF)

    @pl.when(jnp.logical_and(s > 0, s <= steps))
    def _():
        q = s - 1
        g0 = q * group
        acc = jnp.zeros((group * OP, BLK), F32)
        for k in range(K):
            for part in range(2):
                lhs = proj[k, pl.ds(g0 + part, group)].reshape(group * OP, BLK)
                acc = acc + jnp.dot(
                    lhs, band[k, part * BLK : (part + 1) * BLK, :], preferred_element_type=F32
                )
        for g in range(group):
            piece = acc[g * OP : g * OP + O]
            both = jnp.concatenate([piece[:, :HALF], piece[:, HALF:]], axis=0)
            dec[q, g * 2 * O : (g + 1) * 2 * O, :] = both.astype(BF16)
        for off in range(1, n):
            first(q, off).start()

    @pl.when(s > 1)
    def _():
        q = s - 2
        for t in range(2 * group):
            flat[t * O : (t + 1) * O, :] = obs[:, t * HALF : (t + 1) * HALF]
        for off in range(1, n):
            first(q, off).wait_recv()
        lat_row = jnp.broadcast_to(lat[0:1, :], (16, HALF))

        def smooth(diff):
            return diff * lax.rsqrt(diff * diff + SMOOTH * SMOOTH)

        def one(step, carry):
            at = pl.multiple_of(step * 16, 16)
            here = pl.ds(pl.multiple_of(own + at, 16), 16)
            values = [dec[q, here, :].astype(F32)]
            values += [recv[q, off, pl.ds(at, 16), :].astype(F32) for off in range(1, n)]
            sums = [None] * n
            for a in range(n):
                for b in range(a + 1, n):
                    pair = smooth(values[a] - values[b])
                    sums[a] = pair if sums[a] is None else sums[a] + pair
                    sums[b] = -pair if sums[b] is None else sums[b] - pair
            target = flat[here, :]
            for a in range(n):
                slope = smooth(values[a] - target) - sums[a] * (1.0 / (n - 1))
                result = (slope * lat_row).astype(BF16)
                if a == 0:
                    cot[q, here, :] = result
                else:
                    send[q, a, pl.ds(at, 16), :] = result
            return carry

        lax.fori_loop(0, share // 16, one, 0)
        for off in range(1, n):
            second(q, off).start()

    @pl.when(s == steps + 1)
    def _():
        for q in range(steps):
            for off in range(1, n):
                first(q, off).wait_send()
                second(q, off).wait()
        for q in range(steps):
            out[q * n * share : (q + 1) * n * share, :] = cot[q]


def forward(n, feat, left, right, weight, table, obs, lat, group, steps, share):
    chan = feat.shape[0]
    wide = group * BLK
    rows = n * share
    sem = pltpu.SemaphoreType.DMA((steps, n))
    return pl.pallas_call(
        functools.partial(forward_kernel, n, group, steps, share),
        out_shape=jax.ShapeDtypeStruct((steps * rows, HALF), BF16),
        grid=(steps + 2,),
        in_specs=[
            pl.BlockSpec((chan, wide), lambda s: (0, jnp.minimum(s, steps - 1))),
            whole(left.shape),
            whole(right.shape),
            whole(weight.shape),
            whole(table.shape),
            pl.BlockSpec((O, wide), lambda s: (0, jnp.clip(s - 2, 0, steps - 1))),
            whole(lat.shape),
        ],
        out_specs=whole((steps * rows, HALF)),
        scratch_shapes=[
            pltpu.VMEM((K * OP, chan), BF16),
            pltpu.VMEM((K, 2 * BLK, BLK), BF16),
            pltpu.VMEM((K, steps * group + 1, OP, BLK), BF16),
            pltpu.VMEM((steps, rows, HALF), BF16),
            pltpu.VMEM((rows, HALF), F32),
            pltpu.VMEM((steps, n, share, HALF), BF16),
            pltpu.VMEM((steps, n, share, HALF), BF16),
            pltpu.VMEM((steps, rows, HALF), BF16),
            sem,
            sem,
            sem,
            sem,
        ],
        compiler_params=pltpu.CompilerParams(
            collective_id=0, has_side_effects=True, vmem_limit_bytes=VMEM_LIMIT
        ),
        name="forward_slopes",
    )(feat, left, right, weight, table, obs, lat)


WG_ROWS = 2048
WG_PART = 656


def backward_kernel(
    group, steps, share, cells, padded,
    cot, left, right, weight, table, feat, grad, wgrad,
    weight_t, band, ext, spread, acc,
):
    s = pl.program_id(0)
    blocks = steps * group

    @pl.when(s == 0)
    def _():
        ext[:, O:, :] = jnp.zeros((blocks + 1, OP - O, BLK), BF16)
        ext[0, :O, :HALF] = left[...]
        ext[blocks, :O, HALF:] = right[...]

        weight_t[...] = padded_weight(weight).T.astype(BF16)
        build_band(table, band)

        def one(b, carry):
            start = lax.div(b, group) * share + lax.rem(b, group) * (2 * O)
            pair = cot[pl.ds(pl.multiple_of(start, 16), 2 * O), :].astype(F32)
            ext[b, :O, HALF:] = pair[:O].astype(BF16)
            ext[b + 1, :O, :HALF] = pair[O:].astype(BF16)
            return carry

        lax.fori_loop(0, blocks, one, 0)
        acc[...] = jnp.zeros_like(acc)

    g0 = s * group
    for k in range(K):
        got = jnp.zeros((group * OP, BLK), F32)
        for part in range(2):
            lhs = ext[pl.ds(g0 + part, group)].reshape(group * OP, BLK)
            got = got + jnp.dot(
                lhs, band[k, part * BLK : (part + 1) * BLK, :], preferred_element_type=F32
            )
        if padded:
            row = lax.broadcasted_iota(jnp.int32, got.shape, 0) // OP
            lane = lax.broadcasted_iota(jnp.int32, got.shape, 1)
            got = jnp.where((g0 + row) * BLK + lane < cells, got, 0.0)
        got = got.astype(BF16)
        for g in range(group):
            spread[k * OP : (k + 1) * OP, g * BLK : (g + 1) * BLK] = got[g * OP : (g + 1) * OP]

    acc[...] += lax.dot_general(
        spread[...], feat[...], (((1,), (1,)), ((), ())), preferred_element_type=F32
    )

    def one_grad(n, carry):
        lanes = pl.ds(pl.multiple_of(n * BLK, BLK), BLK)
        grad[:, lanes] = jnp.dot(
            weight_t[...], spread[:, lanes], preferred_element_type=F32
        ).astype(BF16)
        return carry

    lax.fori_loop(0, group, one_grad, 0)

    @pl.when(s == steps - 1)
    def _():
        parts = acc.shape[1] // HALF
        wgrad[parts * WG_PART - 16 :, :] = jnp.zeros((WG_ROWS - parts * WG_PART + 16, HALF), BF16)
        for t in range(parts):
            rows = [
                acc[k * OP : k * OP + O, t * HALF : (t + 1) * HALF] for k in range(K)
            ] + [jnp.zeros((8, HALF), F32)]
            wgrad[t * WG_PART : (t + 1) * WG_PART, :] = jnp.concatenate(rows, axis=0).astype(BF16)


def backward(cot, left, right, weight, table, feat, group, steps, cells):
    chan = feat.shape[0]
    wide = group * BLK
    blocks = steps * group
    return pl.pallas_call(
        functools.partial(
            backward_kernel, group, steps, cot.shape[0] // steps, cells, cells != blocks * BLK
        ),
        out_shape=(
            jax.ShapeDtypeStruct(feat.shape, BF16),
            jax.ShapeDtypeStruct((WG_ROWS, HALF), BF16),
        ),
        grid=(steps,),
        in_specs=[
            whole(cot.shape),
            whole(left.shape),
            whole(right.shape),
            whole(weight.shape),
            whole(table.shape),
            pl.BlockSpec((chan, wide), lambda s: (0, s)),
        ],
        out_specs=(pl.BlockSpec((chan, wide), lambda s: (0, s)), whole((WG_ROWS, HALF))),
        scratch_shapes=[
            pltpu.VMEM((chan, K * OP), BF16),
            pltpu.VMEM((K, 2 * BLK, BLK), BF16),
            pltpu.VMEM((blocks + 1, OP, BLK), BF16),
            pltpu.VMEM((K * OP, wide), BF16),
            pltpu.VMEM((K * OP, chan), F32),
        ],
        compiler_params=pltpu.CompilerParams(vmem_limit_bytes=VMEM_LIMIT),
        name="backward_conv",
    )(cot, left, right, weight, table, feat)


def reduce_kernel(ne, nl, scale, part, out, recv1, mid, recv2, got, *sems):
    (ss1, rs1, ss2, rs2, ss3, rs3, ss4, rs4) = sems
    me = lax.axis_index("ens")
    at = lax.axis_index("lon")
    rows = WG_ROWS // ne
    small = rows // nl
    ens_peers = [{"ens": lax.rem(me + off, ne)} for off in range(1, ne)]
    lon_peers = [{"lon": lax.rem(at + off, nl)} for off in range(1, nl)]
    greet(ens_peers + lon_peers)

    def run(copies):
        for copy in copies:
            copy.start()
        for copy in copies:
            copy.wait()

    def send(src, dst, ssem, rsem, peer):
        return pltpu.make_async_remote_copy(
            src_ref=src, dst_ref=dst, send_sem=ssem, recv_sem=rsem, device_id=peer, device_id_type=MESH
        )

    own = pl.multiple_of(me * rows, 16)
    mine = pl.multiple_of(at * small, 8)
    run(
        [
            send(
                part.at[pl.ds(pl.multiple_of(lax.rem(me + off, ne) * rows, 16), rows)],
                recv1.at[off],
                ss1.at[off],
                rs1.at[off],
                {"ens": lax.rem(me + off, ne)},
            )
            for off in range(1, ne)
        ]
    )
    total = part[pl.ds(own, rows), :].astype(F32)
    for off in range(1, ne):
        total = total + recv1[off].astype(F32)
    mid[...] = total
    run(
        [
            send(
                mid.at[pl.ds(pl.multiple_of(lax.rem(at + off, nl) * small, 8), small)],
                recv2.at[off],
                ss2.at[off],
                rs2.at[off],
                {"lon": lax.rem(at + off, nl)},
            )
            for off in range(1, nl)
        ]
    )
    total = mid[pl.ds(mine, small), :]
    for off in range(1, nl):
        total = total + recv2[off]
    recv2[0] = total
    gat = got[1]
    gat[pl.ds(mine, small), :] = total
    run(
        [
            send(
                recv2.at[0],
                gat.at[pl.ds(mine, small)],
                ss3.at[off],
                rs3.at[off],
                {"lon": lax.rem(at + off, nl)},
            )
            for off in range(1, nl)
        ]
    )
    full = got[0]
    full[pl.ds(own, rows), :] = gat[...].astype(BF16)
    run(
        [
            send(
                full.at[pl.ds(own, rows)],
                full.at[pl.ds(own, rows)],
                ss4.at[off],
                rs4.at[off],
                {"ens": lax.rem(me + off, ne)},
            )
            for off in range(1, ne)
        ]
    )
    for t in range(out.shape[1] // HALF):
        piece = full[t * WG_PART : (t + 1) * WG_PART, :].astype(F32) * scale
        out[:, t * HALF : (t + 1) * HALF] = piece[: K * O]


def reduced(ne, nl, scale, part, chan):
    vmem = pl.BlockSpec(memory_space=pltpu.VMEM)
    rows = WG_ROWS // ne
    small = rows // nl

    def body(part, out, recv1, mid, recv2, full, gat, *sems):
        reduce_kernel(ne, nl, scale, part, out, recv1, mid, recv2, (full, gat), *sems)

    return pl.pallas_call(
        body,
        out_shape=jax.ShapeDtypeStruct((K * O, chan), F32),
        in_specs=[vmem],
        out_specs=vmem,
        scratch_shapes=[
            pltpu.VMEM((ne, rows, HALF), BF16),
            pltpu.VMEM((rows, HALF), F32),
            pltpu.VMEM((nl, small, HALF), F32),
            pltpu.VMEM((WG_ROWS, HALF), BF16),
            pltpu.VMEM((rows, HALF), F32),
        ]
        + [pltpu.SemaphoreType.DMA((n,)) for n in (ne, ne, nl, nl, nl, nl, ne, ne)],
        compiler_params=pltpu.CompilerParams(
            collective_id=1, has_side_effects=True, vmem_limit_bytes=VMEM_LIMIT
        ),
        name="weight_reduce",
    )(part)


def passed_along(value, axis, steps):
    count = lax.axis_size(axis)
    return lax.ppermute(value, axis, [(i, (i + steps) % count) for i in range(count)])


def shards(features, proj_weight, basis_vals, row_of, col_off, observed, lat_weight):
    ne = lax.axis_size("ens")
    nl = lax.axis_size("lon")
    assert features.shape[0] == 1
    feat = features[0]
    chan, cells = feat.shape
    aligned = cells % BLK == 0
    blocks = cells // BLK if aligned else pl.cdiv(cells + HALF, BLK)
    group = max(g for g in range(1, 10) if blocks % g == 0)
    steps = blocks // group
    real = group * 2 * O
    share = pl.cdiv(pl.cdiv(real, ne), 16) * 16
    rows = ne * share
    extra = blocks * BLK - cells

    left = passed_along(feat[:, cells - HALF :], "lon", 1)
    right = passed_along(feat[:, :HALF], "lon", -1)
    ahead, back = side_tables(kernel_rows(basis_vals, row_of, col_off))
    if not aligned:
        feat = jnp.pad(jnp.concatenate([feat, right], axis=1), ((0, 0), (0, extra - HALF)))
        right = jnp.zeros_like(right)
        observed = jnp.pad(observed, ((0, 0), (0, extra)))
    lat = jnp.broadcast_to(jnp.tile(lat_weight, HALF // LAT)[None, :], (8, HALF))
    cot = forward(
        ne, feat, left, right, proj_weight, ahead, observed, lat, group, steps, share
    )

    if aligned:
        last = (steps - 1) * rows + real
        cot_left = passed_along(cot[last - O : last], "lon", 1)
        cot_right = passed_along(cot[:O], "lon", -1)
    else:
        flat = cot.reshape(steps, rows, HALF)[:, :real].reshape(2 * blocks, O, HALF)
        flat = flat.transpose(1, 0, 2).reshape(O, blocks * BLK)[:, :cells]
        cot_left = passed_along(flat[:, cells - HALF :], "lon", 1)
        cot_right = passed_along(flat[:, :HALF], "lon", -1)
        flat = jnp.pad(
            jnp.concatenate([flat, cot_right], axis=1), ((0, 0), (0, extra - HALF))
        )
        flat = flat.reshape(O, 2 * blocks, HALF).transpose(1, 0, 2).reshape(steps, real, HALF)
        cot = jnp.pad(flat, ((0, 0), (0, rows - real), (0, 0))).reshape(steps * rows, HALF)
        cot_right = jnp.zeros_like(cot_right)
    grad, part = backward(cot, cot_left, cot_right, proj_weight, back, feat, group, steps, cells)
    scale = 1.0 / math.sqrt(ne * (cells // LAT) * nl * LAT)
    weight_grad = reduced(ne, nl, scale, part, chan)
    return (grad[:, :cells][None], weight_grad)


def solution(mesh):
    in_specs = (P("ens", None, "lon"), P(), P(), P(), P(), P(None, "lon"), P())
    out_specs = (P("ens", None, "lon"), P())
    return jax.shard_map(shards, mesh=mesh, in_specs=in_specs, out_specs=out_specs, check_vma=False)
```

```python
import functools
import math

import jax
import jax.numpy as jnp
from jax import lax
from jax.experimental import pallas as pl
from jax.experimental.pallas import tpu as pltpu
from jax.sharding import PartitionSpec as P

O = 72
OP = 80
K = 9
R = 4
LAT = 32
SMOOTH = 0.25
BLK = 256
HALF = 128
F32 = jnp.float32
BF16 = jnp.bfloat16
MESH = pl.DeviceIdType.MESH
VMEM_LIMIT = 60 * 1024 * 1024


def whole(shape):
    return pl.BlockSpec(shape, lambda s: (0,) * len(shape))


def kernel_rows(basis_vals, row_of, col_off):
    code = (col_off + R) * LAT + row_of
    ids = jnp.arange((2 * R + 1) * LAT, dtype=jnp.int32)
    hit = (code[:, :, None] == ids[None, None, :]).astype(F32)
    table = jnp.einsum("isk,isq->ikq", basis_vals, hit, precision=lax.Precision.HIGHEST)
    return table.astype(BF16)


def side_tables(table):
    taps = 2 * R + 1
    four = table.reshape(LAT, K, taps, LAT)
    ahead = four.transpose(1, 2, 3, 0).reshape(K, taps * LAT, LAT)
    back = four[:, :, ::-1].transpose(1, 2, 0, 3).reshape(K, taps * LAT, LAT)
    return ahead, back


def build_band(table, band):
    lane = lax.broadcasted_iota(jnp.int32, (LAT, BLK), 1)
    spread_lanes = (lane % LAT == lax.broadcasted_iota(jnp.int32, (LAT, BLK), 0)).astype(F32)
    spread_lanes = spread_lanes.astype(BF16)
    place = lane // LAT
    cols = BLK // LAT

    def one(k, carry):
        tiled = jnp.dot(table[k], spread_lanes, preferred_element_type=F32)
        for e in range(2 * cols):
            block = jnp.zeros((LAT, BLK), F32)
            for j in range(cols):
                d = e - j
                if 0 <= d <= 2 * R:
                    block = jnp.where(place == j, tiled[d * LAT : (d + 1) * LAT], block)
            band[k, e * LAT : (e + 1) * LAT, :] = block.astype(BF16)
        return carry

    lax.fori_loop(0, K, one, 0)


def padded_weight(weight):
    wide = weight[...].astype(F32)
    gap = jnp.zeros((OP - O, wide.shape[1]), F32)
    rows = []
    for k in range(K):
        rows += [wide[k * O : (k + 1) * O], gap]
    return jnp.concatenate(rows, axis=0)


def greet(peers):
    barrier = pltpu.get_barrier_semaphore()
    for peer in peers:
        pl.semaphore_signal(barrier, inc=1, device_id=peer, device_id_type=MESH)
    pl.semaphore_wait(barrier, len(peers))


def forward_kernel(
    n, nl, group, steps, share,
    feat, tail, head, weight, table, obs, lat, out, rims,
    wpad, band, proj, dec, flat, recv, send, cot, left, right, rim_left, rim_right,
    ssem1, rsem1, ssem2, rsem2, hsend, hrecv,
):
    s = pl.program_id(0)
    me = lax.axis_index("ens")
    real = group * 2 * O
    own = pl.multiple_of(me * share, 16)
    after = {"lon": lax.rem(lax.axis_index("lon") + 1, nl)}
    before = {"lon": lax.rem(lax.axis_index("lon") + nl - 1, nl)}

    def rim(src, dst, slot, peer):
        return pltpu.make_async_remote_copy(
            src_ref=src,
            dst_ref=dst,
            send_sem=hsend.at[slot],
            recv_sem=hrecv.at[slot],
            device_id=peer,
            device_id_type=MESH,
        )

    def first(q, off):
        peer = lax.rem(me + off, n)
        return pltpu.make_async_remote_copy(
            src_ref=dec.at[q, pl.ds(pl.multiple_of(peer * share, 16), share)],
            dst_ref=recv.at[q, off],
            send_sem=ssem1.at[q, off],
            recv_sem=rsem1.at[q, off],
            device_id={"ens": peer},
            device_id_type=MESH,
        )

    def second(q, off):
        return pltpu.make_async_remote_copy(
            src_ref=send.at[q, off],
            dst_ref=cot.at[q, pl.ds(own, share)],
            send_sem=ssem2.at[q, off],
            recv_sem=rsem2.at[q, off],
            device_id={"ens": lax.rem(me - off + n, n)},
            device_id_type=MESH,
        )

    def put(values, h, lo):
        for k in range(K):
            proj[k, h, :, lo : lo + HALF] = values[k * OP : (k + 1) * OP].astype(BF16)

    @pl.when(s == 0)
    def _():
        greet([{"ens": lax.rem(me + off, n)} for off in range(1, n)] + [after, before])
        rim(tail, left, 0, after).start()
        rim(head, right, 1, before).start()
        wpad[...] = padded_weight(weight).astype(BF16)
        build_band(table, band)
        if n * share > real:
            for q in range(steps):
                dec[q, real:, :] = jnp.zeros((n * share - real, HALF), BF16)
            flat[real:, :] = jnp.zeros((n * share - real, HALF), F32)

    @pl.when(s < steps)
    def _():
        def one(b, carry):
            lanes = pl.ds(pl.multiple_of(b * BLK, BLK), BLK)
            got = jnp.dot(wpad[...], feat[:, lanes], preferred_element_type=F32)
            h = s * group + b
            put(got[:, :HALF], h, HALF)
            put(got[:, HALF:], h + 1, 0)
            return carry

        lax.fori_loop(0, group, one, 0)

    @pl.when(s == 1)
    def _():
        rim(tail, left, 0, after).wait()
        put(jnp.dot(wpad[...], left[...], preferred_element_type=F32), 0, 0)

    @pl.when(s == steps)
    def _():
        rim(head, right, 1, before).wait()
        put(jnp.dot(wpad[...], right[...], preferred_element_type=F32), steps * group, HALF)

    @pl.when(jnp.logical_and(s > 0, s <= steps))
    def _():
        q = s - 1
        g0 = q * group
        acc = jnp.zeros((group * OP, BLK), F32)
        for k in range(K):
            for part in range(2):
                lhs = proj[k, pl.ds(g0 + part, group)].reshape(group * OP, BLK)
                acc = acc + jnp.dot(
                    lhs, band[k, part * BLK : (part + 1) * BLK, :], preferred_element_type=F32
                )
        for g in range(group):
            piece = acc[g * OP : g * OP + O]
            both = jnp.concatenate([piece[:, :HALF], piece[:, HALF:]], axis=0)
            dec[q, g * 2 * O : (g + 1) * 2 * O, :] = both.astype(BF16)
        for off in range(1, n):
            first(q, off).start()

    @pl.when(s > 1)
    def _():
        q = s - 2
        for t in range(2 * group):
            flat[t * O : (t + 1) * O, :] = obs[:, t * HALF : (t + 1) * HALF]
        for off in range(1, n):
            first(q, off).wait_recv()
        lat_row = jnp.broadcast_to(lat[0:1, :], (16, HALF))

        def smooth(diff):
            return diff * lax.rsqrt(diff * diff + SMOOTH * SMOOTH)

        def one(step, carry):
            at = pl.multiple_of(step * 16, 16)
            here = pl.ds(pl.multiple_of(own + at, 16), 16)
            values = [dec[q, here, :].astype(F32)]
            values += [recv[q, off, pl.ds(at, 16), :].astype(F32) for off in range(1, n)]
            sums = [None] * n
            for a in range(n):
                for b in range(a + 1, n):
                    pair = smooth(values[a] - values[b])
                    sums[a] = pair if sums[a] is None else sums[a] + pair
                    sums[b] = -pair if sums[b] is None else sums[b] - pair
            target = flat[here, :]
            for a in range(n):
                slope = smooth(values[a] - target) - sums[a] * (1.0 / (n - 1))
                result = (slope * lat_row).astype(BF16)
                if a == 0:
                    cot[q, here, :] = result
                else:
                    send[q, a, pl.ds(at, 16), :] = result
            return carry

        lax.fori_loop(0, share // 16, one, 0)
        for off in range(1, n):
            second(q, off).start()

    @pl.when(s == steps + 1)
    def _():
        for q in range(steps):
            for off in range(1, n):
                first(q, off).wait_send()
                second(q, off).wait()
        last = rim(cot.at[steps - 1, pl.ds(real - OP, OP)], rim_left, 2, after)
        opening = rim(cot.at[0, pl.ds(0, OP)], rim_right, 3, before)
        last.start()
        opening.start()
        for q in range(steps):
            out[q * n * share : (q + 1) * n * share, :] = cot[q]
        last.wait()
        opening.wait()
        rims[0] = rim_left[...]
        rims[1] = rim_right[...]


def forward(n, nl, feat, tail, head, weight, table, obs, lat, group, steps, share):
    chan = feat.shape[0]
    wide = group * BLK
    rows = n * share
    sem = pltpu.SemaphoreType.DMA((steps, n))
    return pl.pallas_call(
        functools.partial(forward_kernel, n, nl, group, steps, share),
        out_shape=(
            jax.ShapeDtypeStruct((steps * rows, HALF), BF16),
            jax.ShapeDtypeStruct((2, OP, HALF), BF16),
        ),
        grid=(steps + 2,),
        in_specs=[
            pl.BlockSpec((chan, wide), lambda s: (0, jnp.minimum(s, steps - 1))),
            whole(tail.shape),
            whole(head.shape),
            whole(weight.shape),
            whole(table.shape),
            pl.BlockSpec((O, wide), lambda s: (0, jnp.clip(s - 2, 0, steps - 1))),
            whole(lat.shape),
        ],
        out_specs=(whole((steps * rows, HALF)), whole((2, OP, HALF))),
        scratch_shapes=[
            pltpu.VMEM((K * OP, chan), BF16),
            pltpu.VMEM((K, 2 * BLK, BLK), BF16),
            pltpu.VMEM((K, steps * group + 1, OP, BLK), BF16),
            pltpu.VMEM((steps, rows, HALF), BF16),
            pltpu.VMEM((rows, HALF), F32),
            pltpu.VMEM((steps, n, share, HALF), BF16),
            pltpu.VMEM((steps, n, share, HALF), BF16),
            pltpu.VMEM((steps, rows, HALF), BF16),
            pltpu.VMEM((chan, HALF), BF16),
            pltpu.VMEM((chan, HALF), BF16),
            pltpu.VMEM((OP, HALF), BF16),
            pltpu.VMEM((OP, HALF), BF16),
            sem,
            sem,
            sem,
            sem,
            pltpu.SemaphoreType.DMA((4,)),
            pltpu.SemaphoreType.DMA((4,)),
        ],
        compiler_params=pltpu.CompilerParams(
            collective_id=0, has_side_effects=True, vmem_limit_bytes=VMEM_LIMIT
        ),
        name="forward_slopes",
    )(feat, tail, head, weight, table, obs, lat)


WG_ROWS = 2048
WG_PART = 656


def backward_kernel(
    group, steps, piece, share, cells, padded,
    cot, left, right, weight, table, feat, grad, wgrad,
    weight_t, band, ext, spread, acc,
):
    s = pl.program_id(0)
    blocks = steps * group

    @pl.when(s == 0)
    def _():
        ext[:, O:, :] = jnp.zeros((blocks + 1, OP - O, BLK), BF16)
        ext[0, :O, :HALF] = left[...].astype(F32)[OP - O :].astype(BF16)
        ext[blocks, :O, HALF:] = right[:O]

        weight_t[...] = padded_weight(weight).T.astype(BF16)
        build_band(table, band)

        def one(b, carry):
            start = lax.div(b, piece) * share + lax.rem(b, piece) * (2 * O)
            pair = cot[pl.ds(pl.multiple_of(start, 16), 2 * O), :].astype(F32)
            ext[b, :O, HALF:] = pair[:O].astype(BF16)
            ext[b + 1, :O, :HALF] = pair[O:].astype(BF16)
            return carry

        lax.fori_loop(0, blocks, one, 0)
        acc[...] = jnp.zeros_like(acc)

    g0 = s * group
    for k in range(K):
        got = jnp.zeros((group * OP, BLK), F32)
        for part in range(2):
            lhs = ext[pl.ds(g0 + part, group)].reshape(group * OP, BLK)
            got = got + jnp.dot(
                lhs, band[k, part * BLK : (part + 1) * BLK, :], preferred_element_type=F32
            )
        if padded:
            row = lax.broadcasted_iota(jnp.int32, got.shape, 0) // OP
            lane = lax.broadcasted_iota(jnp.int32, got.shape, 1)
            got = jnp.where((g0 + row) * BLK + lane < cells, got, 0.0)
        got = got.astype(BF16)
        for g in range(group):
            spread[k * OP : (k + 1) * OP, g * BLK : (g + 1) * BLK] = got[g * OP : (g + 1) * OP]

    acc[...] += lax.dot_general(
        spread[...], feat[...], (((1,), (1,)), ((), ())), preferred_element_type=F32
    )

    def one_grad(n, carry):
        lanes = pl.ds(pl.multiple_of(n * BLK, BLK), BLK)
        grad[:, lanes] = jnp.dot(
            weight_t[...], spread[:, lanes], preferred_element_type=F32
        ).astype(BF16)
        return carry

    lax.fori_loop(0, group, one_grad, 0)

    @pl.when(s == steps - 1)
    def _():
        parts = acc.shape[1] // HALF
        wgrad[parts * WG_PART - 16 :, :] = jnp.zeros((WG_ROWS - parts * WG_PART + 16, HALF), BF16)
        for t in range(parts):
            rows = [
                acc[k * OP : k * OP + O, t * HALF : (t + 1) * HALF] for k in range(K)
            ] + [jnp.zeros((8, HALF), F32)]
            wgrad[t * WG_PART : (t + 1) * WG_PART, :] = jnp.concatenate(rows, axis=0).astype(BF16)


def backward(cot, left, right, weight, table, feat, group, steps, piece, cells):
    chan = feat.shape[0]
    wide = group * BLK
    blocks = steps * group
    return pl.pallas_call(
        functools.partial(
            backward_kernel,
            group,
            steps,
            piece,
            cot.shape[0] * piece // blocks,
            cells,
            cells != blocks * BLK,
        ),
        out_shape=(
            jax.ShapeDtypeStruct(feat.shape, BF16),
            jax.ShapeDtypeStruct((WG_ROWS, HALF), BF16),
        ),
        grid=(steps,),
        in_specs=[
            whole(cot.shape),
            whole(left.shape),
            whole(right.shape),
            whole(weight.shape),
            whole(table.shape),
            pl.BlockSpec((chan, wide), lambda s: (0, s)),
        ],
        out_specs=(pl.BlockSpec((chan, wide), lambda s: (0, s)), whole((WG_ROWS, HALF))),
        scratch_shapes=[
            pltpu.VMEM((chan, K * OP), BF16),
            pltpu.VMEM((K, 2 * BLK, BLK), BF16),
            pltpu.VMEM((blocks + 1, OP, BLK), BF16),
            pltpu.VMEM((K * OP, wide), BF16),
            pltpu.VMEM((K * OP, chan), F32),
        ],
        compiler_params=pltpu.CompilerParams(vmem_limit_bytes=VMEM_LIMIT),
        name="backward_conv",
    )(cot, left, right, weight, table, feat)


def reduce_kernel(ne, nl, scale, part, out, recv1, mid, recv2, got, *sems):
    (ss1, rs1, ss2, rs2, ss3, rs3, ss4, rs4) = sems
    me = lax.axis_index("ens")
    at = lax.axis_index("lon")
    rows = WG_ROWS // ne
    small = rows // nl
    ens_peers = [{"ens": lax.rem(me + off, ne)} for off in range(1, ne)]
    lon_peers = [{"lon": lax.rem(at + off, nl)} for off in range(1, nl)]
    greet(ens_peers + lon_peers)

    def run(copies):
        for copy in copies:
            copy.start()
        for copy in copies:
            copy.wait()

    def send(src, dst, ssem, rsem, peer):
        return pltpu.make_async_remote_copy(
            src_ref=src, dst_ref=dst, send_sem=ssem, recv_sem=rsem, device_id=peer, device_id_type=MESH
        )

    own = pl.multiple_of(me * rows, 16)
    mine = pl.multiple_of(at * small, 8)
    run(
        [
            send(
                part.at[pl.ds(pl.multiple_of(lax.rem(me + off, ne) * rows, 16), rows)],
                recv1.at[off],
                ss1.at[off],
                rs1.at[off],
                {"ens": lax.rem(me + off, ne)},
            )
            for off in range(1, ne)
        ]
    )
    total = part[pl.ds(own, rows), :].astype(F32)
    for off in range(1, ne):
        total = total + recv1[off].astype(F32)
    mid[...] = total
    run(
        [
            send(
                mid.at[pl.ds(pl.multiple_of(lax.rem(at + off, nl) * small, 8), small)],
                recv2.at[off],
                ss2.at[off],
                rs2.at[off],
                {"lon": lax.rem(at + off, nl)},
            )
            for off in range(1, nl)
        ]
    )
    total = mid[pl.ds(mine, small), :]
    for off in range(1, nl):
        total = total + recv2[off]
    recv2[0] = total
    gat = got[1]
    gat[pl.ds(mine, small), :] = total
    run(
        [
            send(
                recv2.at[0],
                gat.at[pl.ds(mine, small)],
                ss3.at[off],
                rs3.at[off],
                {"lon": lax.rem(at + off, nl)},
            )
            for off in range(1, nl)
        ]
    )
    full = got[0]
    full[pl.ds(own, rows), :] = gat[...].astype(BF16)
    run(
        [
            send(
                full.at[pl.ds(own, rows)],
                full.at[pl.ds(own, rows)],
                ss4.at[off],
                rs4.at[off],
                {"ens": lax.rem(me + off, ne)},
            )
            for off in range(1, ne)
        ]
    )
    for t in range(out.shape[1] // HALF):
        piece = full[t * WG_PART : (t + 1) * WG_PART, :].astype(F32) * scale
        out[:, t * HALF : (t + 1) * HALF] = piece[: K * O]


def reduced(ne, nl, scale, part, chan):
    vmem = pl.BlockSpec(memory_space=pltpu.VMEM)
    rows = WG_ROWS // ne
    small = rows // nl

    def body(part, out, recv1, mid, recv2, full, gat, *sems):
        reduce_kernel(ne, nl, scale, part, out, recv1, mid, recv2, (full, gat), *sems)

    return pl.pallas_call(
        body,
        out_shape=jax.ShapeDtypeStruct((K * O, chan), F32),
        in_specs=[vmem],
        out_specs=vmem,
        scratch_shapes=[
            pltpu.VMEM((ne, rows, HALF), BF16),
            pltpu.VMEM((rows, HALF), F32),
            pltpu.VMEM((nl, small, HALF), F32),
            pltpu.VMEM((WG_ROWS, HALF), BF16),
            pltpu.VMEM((rows, HALF), F32),
        ]
        + [pltpu.SemaphoreType.DMA((n,)) for n in (ne, ne, nl, nl, nl, nl, ne, ne)],
        compiler_params=pltpu.CompilerParams(
            collective_id=1, has_side_effects=True, vmem_limit_bytes=VMEM_LIMIT
        ),
        name="weight_reduce",
    )(part)


def passed_along(value, axis, steps):
    count = lax.axis_size(axis)
    return lax.ppermute(value, axis, [(i, (i + steps) % count) for i in range(count)])


def shards(features, proj_weight, basis_vals, row_of, col_off, observed, lat_weight):
    ne = lax.axis_size("ens")
    nl = lax.axis_size("lon")
    assert features.shape[0] == 1
    feat = features[0]
    chan, cells = feat.shape
    aligned = cells % BLK == 0
    blocks = cells // BLK if aligned else pl.cdiv(cells + HALF, BLK)
    group_back = max(g for g in range(1, 10) if blocks % g == 0)
    steps_back = blocks // group_back
    group = max(g for g in range(1, 7) if blocks % g == 0)
    steps = blocks // group
    real = group * 2 * O
    share = pl.cdiv(pl.cdiv(real, ne), 16) * 16
    rows = ne * share
    extra = blocks * BLK - cells

    tail = feat[:, cells - HALF :]
    head = feat[:, :HALF]
    ahead, back = side_tables(kernel_rows(basis_vals, row_of, col_off))
    if not aligned:
        right = passed_along(head, "lon", -1)
        feat = jnp.pad(jnp.concatenate([feat, right], axis=1), ((0, 0), (0, extra - HALF)))
        observed = jnp.pad(observed, ((0, 0), (0, extra)))
    lat = jnp.broadcast_to(jnp.tile(lat_weight, HALF // LAT)[None, :], (8, HALF))
    cot, rims = forward(
        ne, nl, feat, tail, head, proj_weight, ahead, observed, lat, group, steps, share
    )

    if aligned:
        cot_left, cot_right = rims[0], rims[1]
    else:
        flat = cot.reshape(steps, rows, HALF)[:, :real].reshape(2 * blocks, O, HALF)
        flat = flat.transpose(1, 0, 2).reshape(O, blocks * BLK)[:, :cells]
        cot_left = passed_along(flat[:, cells - HALF :], "lon", 1)
        cot_right = passed_along(flat[:, :HALF], "lon", -1)
        flat = jnp.pad(
            jnp.concatenate([flat, cot_right], axis=1), ((0, 0), (0, extra - HALF))
        )
        flat = flat.reshape(O, 2 * blocks, HALF).transpose(1, 0, 2).reshape(steps, real, HALF)
        cot = jnp.pad(flat, ((0, 0), (0, rows - real), (0, 0))).reshape(steps * rows, HALF)
        cot_left = jnp.pad(cot_left, ((OP - O, 0), (0, 0)))
        cot_right = jnp.zeros((OP, HALF), BF16)
    grad, part = backward(
        cot, cot_left, cot_right, proj_weight, back, feat, group_back, steps_back, group, cells
    )
    scale = 1.0 / math.sqrt(ne * (cells // LAT) * nl * LAT)
    weight_grad = reduced(ne, nl, scale, part, chan)
    return (grad[:, :cells][None], weight_grad)


def solution(mesh):
    in_specs = (P("ens", None, "lon"), P(), P(), P(), P(), P(None, "lon"), P())
    out_specs = (P("ens", None, "lon"), P())
    return jax.shard_map(shards, mesh=mesh, in_specs=in_specs, out_specs=out_specs, check_vma=False)
```
